128 devices in a mesh: rep: 16 (over x_lo, y, core), fsdp: 8 (over x_hi, z).
Axes of the slice: x: 4 (x_hi: 2, x_lo: 2; x = x_hi * 2 + x_lo), y: 4, z: 4, core: 2. Of those that a mesh axis runs over, the one named last changes fastest.
Arguments:
- tokens: bfloat16 [131072, 8192], P(('rep', 'fsdp')), may hold values from -6 to 6
- norm_gain: bfloat16 [8192], replicated, may hold values from 0.25 to 1.75
- deltas: bfloat16 [16, 8192, 1024], P('rep', 'fsdp'), may hold values from -0.09375 to 0.09375
- inner_steps: int32 [16, 16], replicated, may hold values from 1 to 64
- bucket_of_row: int32 [8192], P('fsdp'), may hold values from 0 to 15, never falling along the last dimension, each value on 1 to 1024 neighbouring positions
- master: float32 [8192, 1024], P(('fsdp', 'rep')), may hold values from -0.0625 to 0.0625
- momentum: float32 [8192, 1024], P(('fsdp', 'rep')), may hold values from -0.0625 to 0.0625
Outputs:
- keys: bfloat16 [131072, 1024], P(('rep', 'fsdp'))
- master_new: float32 [8192, 1024], P(('fsdp', 'rep'))
- momentum_new: float32 [8192, 1024], P(('fsdp', 'rep'))
The draws below stay inside these ranges and needn't reach their ends.
Inputs may be any that keep to these rules, and one draw needn't show every extreme that they name: `bucket_of_row`: never falls along the rows; each bucket holds 1 to 1024 rows.
All inputs are finite; a program needn't handle non-finite values.
Results may differ from the reference program's by a relative error of at most 0.0058.
Values may be sent and summed in bfloat16 or wider, within the bound.
A program may use at most 192 MiB of HBM per device.

```python
import math
import jax
import jax.numpy as jnp
import numpy as np
from jax import lax

D = 8192
KV = 1024
TOK_DEV = 1024
NB = 16
REPS = 16
TOKENS = 131072
BUCKET_MOST = 1024


def touch_ends(values, own_key, low, top_value):
    place = [jax.random.randint(jax.random.fold_in(own_key, axis), (), 0, length) for axis, length in enumerate(values.shape)]
    widest = values.shape.index(max(values.shape))
    neighbour = place[:widest] + [(place[widest] + 1) % values.shape[widest]] + place[widest + 1:]
    return values.at[tuple(place)].set(low).at[tuple(neighbour)].set(top_value)


def raised(drawn, own_key, source, target, parts, factor):
    owner, partner = [(jnp.arange(drawn.shape[axis_at]) // (drawn.shape[axis_at] // parts)).reshape([-1 if axis == axis_at else 1 for axis in range(drawn.ndim)]) for axis_at in (source, target)]
    chosen = jax.random.permutation(own_key, parts)[partner]
    strong = (owner == chosen) | (owner == (partner + parts // 2) % parts)
    return jnp.where(strong, factor * drawn, drawn)


def level_of(rng, shape, pieces, smallest, largest):
    loudness = 1.0
    for dim, blocks in pieces:
        steps = jax.random.uniform(jax.random.fold_in(jax.random.fold_in(rng, 6), dim), (blocks,), jnp.float32, smallest / len(pieces), largest / len(pieces))
        loudness = loudness * jnp.repeat(jnp.exp(steps), shape[dim] // blocks).reshape((-1,) + (1,) * (len(shape) - 1 - dim))
    return loudness


def length_profile(amount, total, most, slope):
    loads = [(1 << 20) // math.isqrt(standing ** slope) + 1 for standing in range(2, amount + 1)]
    surplus, holding = total - most - (amount - 1), [1] * (amount - 1)
    while surplus > 0:
        movable = [i for i in range(amount - 1) if holding[i] < most]
        mass, budget = sum([loads[i] for i in movable]), surplus
        for i in movable:
            more = min(most - holding[i], max(1, budget * loads[i] // mass), surplus)
            holding[i] = holding[i] + more
            surplus = surplus - more
    return np.array([most] + holding)


def uneven_parts(rng, amount, total, limit, slope):
    if amount == 2:
        one = jax.random.randint(rng, (), max(1, total - limit), min(limit, total - 1) + 1)
        return jnp.stack([one, total - one])
    lengths = jnp.asarray(length_profile(amount, total, limit, slope), jnp.int32)
    twos = (amount - 1) // 2
    source_of, taker = lengths[1:1 + 2 * twos:2], lengths[2:2 + 2 * twos:2]
    slack = jnp.minimum(source_of - 1, limit - taker)
    shifted = jax.random.randint(jax.random.fold_in(rng, 1), (twos,), 0, 1 << 20) % (slack + 1)
    lengths = lengths.at[1:1 + 2 * twos:2].set(source_of - shifted).at[2:2 + 2 * twos:2].set(taker + shifted)
    return lengths[jax.random.permutation(jax.random.fold_in(rng, 2), amount)]


def normal_values(own_key, shape, spread, most, split=(), kind=jnp.bfloat16):
    result = spread * jax.random.normal(own_key, shape, jnp.float32)
    if split:
        result = result * level_of(own_key, shape, split, -0.22, 0.18)
    return jnp.clip(result, -most, most).astype(kind)


def noise_with(rng, extent, width, bound, split, heavy, dtype=jnp.bfloat16):
    entries = width * jax.random.normal(rng, extent, jnp.float32)
    if split:
        entries = entries * level_of(rng, extent, split, -0.22, 0.18)
    return jnp.clip(raised(entries, jax.random.fold_in(rng, 3), *heavy), -bound, bound).astype(dtype)


def setup_inputs(seed: int = 0) -> dict:
    splits = jax.random.split(jax.random.key(seed), 8)
    return {
        "tokens": normal_values(splits[0], (TOKENS, D), 1.0, 6.0, ((0, 128),)),
        "norm_gain": jnp.clip(1.0 + 0.15 * jax.random.normal(splits[1], (D,), jnp.float32), 0.25, 1.75).astype(jnp.bfloat16),
        "deltas": noise_with(splits[2], (REPS, D, KV), D ** -0.5, 0.09375, ((0, 16), (1, 8)), (0, 1, 16, 2.0)),
        "inner_steps": touch_ends(jax.random.randint(splits[3], (REPS, NB), 1, 65), jax.random.fold_in(splits[3], 1), 1, 64).astype(jnp.int32),
        "bucket_of_row": jnp.searchsorted(jnp.cumsum(uneven_parts(splits[4], NB, D, BUCKET_MOST, 1)), jnp.arange(D), side="right").astype(jnp.int32),
        "master": normal_values(splits[5], (D, KV), D ** -0.5, 0.0625, ((0, 128),), jnp.float32),
        "momentum": normal_values(splits[6], (D, KV), D ** -0.5, 0.0625, ((0, 128),), jnp.float32),
    }


OUTER_RATE = 0.7
MOMENTUM_KEEP = 0.9
EPSILON = 1e-05

def normalize(rows, norm_gain):
    values = rows.astype(jnp.float32)
    scale = lax.rsqrt(lax.optimization_barrier(jnp.mean(values * values, axis=1, keepdims=True)) + EPSILON)
    return (values * scale * norm_gain.astype(jnp.float32)[None, :]).astype(jnp.bfloat16)

def reference(tokens, norm_gain, deltas, inner_steps, bucket_of_row, master, momentum):
    counts = inner_steps.astype(jnp.float32)
    share = counts / lax.optimization_barrier(jnp.sum(counts, axis=0, keepdims=True))
    row_weight = share[:, bucket_of_row]

    def add_one(total, pair):
        weight_row, delta = pair
        return (total + weight_row[:, None] * delta.astype(jnp.float32), None)
    averaged, _ = lax.scan(add_one, jnp.zeros(master.shape, jnp.float32), (row_weight, deltas))
    momentum_new = MOMENTUM_KEEP * momentum + averaged
    master_new = master - OUTER_RATE * (averaged + MOMENTUM_KEEP * momentum_new)
    layer = master_new.astype(jnp.bfloat16)
    blocks = tokens.reshape(-1, TOK_DEV, tokens.shape[1])

    def project(rows):
        normed = normalize(rows, norm_gain)
        return jnp.dot(normed, layer, preferred_element_type=jnp.float32).astype(jnp.bfloat16)
    keys = lax.map(project, blocks).reshape(tokens.shape[0], layer.shape[1])
    return (keys, master_new, momentum_new)
```

```python
import jax
import jax.numpy as jnp
from jax import lax
from jax.experimental import pallas as pl
from jax.experimental.pallas import tpu as pltpu
from jax.sharding import PartitionSpec as P

OUTER_RATE = 0.7
MOMENTUM_KEEP = 0.9
EPSILON = 1e-05
MESH = pl.DeviceIdType.MESH
F32 = jnp.float32
BF16 = jnp.bfloat16

PARTS = 4
COLS = 256
ROWS = 64
TILE = 256
LINE, PLANE, CUBE, FORWARD, SIBLING, COPIES = 0, 3, 6, 14, 18, 34


def mod4(v):
    return lax.rem(v + 8, 4)


def position():
    rep = lax.axis_index("rep")
    fsdp = lax.axis_index("fsdp")
    x = lax.div(fsdp, 4) * 2 + lax.div(rep, 8)
    y = lax.rem(lax.div(rep, 2), 4)
    z = lax.rem(fsdp, 4)
    return x, y, z, lax.rem(rep, 2)


def device(x, y, z, core):
    return (lax.rem(x, 2) * 8 + y * 2 + core, lax.div(x, 2) * 4 + z)


def choose(axis, x, y, z):
    return lax.div(2 - axis, 2) * x + lax.rem(axis, 2) * y + lax.div(axis, 2) * z


def roles(part):
    return lax.rem(part, 3), lax.rem(part + 1, 3), lax.rem(part + 2, 3)


def kernel(tokens, gain, deltas, steps, bucket, master, momentum,
           keys, master_out, momentum_out,
           tok, layer, acc, own, sib, pairs, landed, mas, mom, gain_v, steps_v, bucket_v,
           wcol, inv, out, local, pair_sem, red_s, red_r, gat_s, gat_r):
    x, y, z, core = position()
    chip = lax.rem(x, 2) * 4 + y
    sibling = device(x, y, z, 1 - core)

    def local_copy(src, dst, i):
        return pltpu.make_async_copy(src, dst, local.at[i])

    own_copy = local_copy(deltas.at[:, core], own, 0)
    steps_copy = local_copy(steps, steps_v, 1)
    bucket_copy = local_copy(bucket, bucket_v, 2)
    gain_copy = local_copy(gain, gain_v, 3)
    mas_copy = local_copy(master, mas, 4)
    mom_copy = local_copy(momentum, mom, 5)
    for copy in (steps_copy, bucket_copy, own_copy, gain_copy, mas_copy, mom_copy):
        copy.start()

    barrier = pltpu.get_barrier_semaphore()
    peers = [sibling]
    for d in range(1, 8):
        k = lax.rem(chip + d, 8)
        peers.append(device(lax.div(x, 2) * 2 + lax.div(k, 4), lax.rem(k, 4), z, core))
    far = (1 - lax.div(x, 2)) * 2
    peers.append(device(far, y, z, core))
    peers.append(device(far + 1, y, z, core))
    for d in range(1, 4):
        peers.append(device(x, y, mod4(z + d), core))
    for peer in peers:
        pl.semaphore_signal(barrier, inc=1, device_id=peer, device_id_type=MESH)
    pl.semaphore_wait(barrier, len(peers))

    pair_copy = pltpu.make_async_remote_copy(
        src_ref=deltas.at[:, 1 - core], dst_ref=sib, send_sem=pair_sem.at[0], recv_sem=pair_sem.at[1],
        device_id=sibling, device_id_type=MESH)
    pair_copy.start()
    tok_copies = [local_copy(tokens.at[pl.ds(i * TILE, TILE)], tok.at[pl.ds(i * TILE, TILE)], 6 + i) for i in range(4)]
    for copy in tok_copies:
        copy.start()

    steps_copy.wait()
    bucket_copy.wait()
    counts = steps_v[...].astype(F32)
    share = counts / jnp.sum(counts, axis=0, keepdims=True)
    replica = lax.axis_index("rep")
    replica_ids = lax.broadcasted_iota(jnp.int32, (16, 16), 0)
    lane = lax.broadcasted_iota(jnp.int32, (ROWS, 128), 1)
    row = lax.broadcasted_iota(jnp.int32, (ROWS, 128), 0)
    mine = lane == row + core * ROWS
    buckets = bucket_v[...]
    for side, who in enumerate((replica, replica + 1 - 2 * core)):
        row_share = jnp.sum(jnp.where(replica_ids == who, share, 0.0), axis=0, keepdims=True)
        weight = jnp.zeros((8, 128), F32)
        for b in range(16):
            weight = weight + jnp.where(buckets == b, row_share[:, b:b + 1], 0.0)
        for k in range(8):
            column = jnp.sum(jnp.where(mine, weight[k:k + 1, :], 0.0), axis=1, keepdims=True)
            wcol[side, k] = jnp.broadcast_to(column, (ROWS, 128))

    own_copy.wait()
    pair_copy.wait()

    def reduce_copy(part, d):
        k = lax.rem(chip + d, 8)
        return pltpu.make_async_remote_copy(
            src_ref=pairs.at[part, k], dst_ref=landed.at[part, d - 1],
            send_sem=red_s.at[part, d - 1], recv_sem=red_r.at[part, d - 1],
            device_id=device(lax.div(x, 2) * 2 + lax.div(k, 4), lax.rem(k, 4), z, core), device_id_type=MESH)

    @pl.loop(0, PARTS)
    def _(part):
        columns = pl.ds(pl.multiple_of(part * COLS, COLS), COLS)

        @pl.loop(0, 8)
        def _(k):
            w0 = wcol[0, k][:, :1]
            w1 = wcol[1, k][:, :1]
            both = w0 * own[k, :, columns].astype(F32) + w1 * sib[k, :, columns].astype(F32)
            pairs[part, k] = both.astype(BF16)

        @pl.loop(1, 8)
        def _(d):
            reduce_copy(part, d).start()

    acc[...] = jnp.zeros_like(acc)
    gain_copy.wait()
    gain_row = gain_v[pl.ds(lax.axis_index("fsdp") * 8 + chip, 1), :]
    gain_col = jnp.sum(jnp.where(mine, gain_row, 0.0), axis=1, keepdims=True)
    mas_copy.wait()
    mom_copy.wait()
    for copy in tok_copies:
        copy.wait()

    @pl.loop(0, 1024 // 32)
    def _(i):
        rows = pl.ds(pl.multiple_of(i * 32, 32), 32)
        total = jnp.zeros((32, 128), F32)
        for j in range(64):
            v = tok[rows, j * 128:(j + 1) * 128].astype(F32)
            total = total + v * v
        mean = jnp.sum(total, axis=1, keepdims=True) * (1.0 / 8192.0)
        inv[rows, :] = jnp.broadcast_to(lax.rsqrt(mean + EPSILON), (32, 128))

    def place(part):
        q1, q2, q3 = roles(part)
        return choose(q1, x, y, z), choose(q2, x, y, z), choose(q3, x, y, z)

    def along(axis, d):
        return device(mod4(x + lax.div(2 - axis, 2) * d), mod4(y + lax.rem(axis, 2) * d), mod4(z + lax.div(axis, 2) * d), core)

    def gather_copy(part, ref, index, target):
        return pltpu.make_async_remote_copy(
            src_ref=ref, dst_ref=ref, send_sem=gat_s.at[part, index], recv_sem=gat_r.at[part, index],
            device_id=target, device_id_type=MESH)

    def line_send(part, d):
        i1, i2, i3 = place(part)
        return gather_copy(part, layer.at[part, i3, i2, i1, core], LINE + d - 1, along(roles(part)[0], d))

    def line_recv(part, d):
        i1, i2, i3 = place(part)
        return gather_copy(part, layer.at[part, i3, i2, mod4(i1 - d), core], LINE + d - 1, sibling)

    def a_line(part, da3, da2, who):
        i1, i2, i3 = place(part)
        return layer.at[part, mod4(i3 + da3), mod4(i2 + da2), :, who]

    def plane_send(part, d):
        return gather_copy(part, a_line(part, 0, 0, core), PLANE + d - 1, along(roles(part)[1], d))

    def plane_recv(part, d):
        return gather_copy(part, a_line(part, 0, -d, core), PLANE + d - 1, sibling)

    def cube_send(part, way, j):
        return gather_copy(part, a_line(part, 0, -j, core), CUBE + way * 4 + j, along(roles(part)[2], 1 - 2 * way))

    def cube_recv(part, way, j):
        return gather_copy(part, a_line(part, 2 * way - 1, -j, core), CUBE + way * 4 + j, sibling)

    def forward_send(part, way, j):
        return gather_copy(part, a_line(part, 2 * way - 1, -j, core), FORWARD + j, along(roles(part)[2], 1 - 2 * way))

    def forward_recv(part, j):
        return gather_copy(part, a_line(part, 2, -j, core), FORWARD + j, sibling)

    SHIFT = (0, -1, 1, 2)

    def sibling_send(part, k, j):
        return gather_copy(part, a_line(part, SHIFT[k], -j, core), SIBLING + k * 4 + j, sibling)

    def sibling_recv(part, k, j):
        return gather_copy(part, a_line(part, SHIFT[k], -j, 1 - core), SIBLING + k * 4 + j, sibling)

    def multiply(part, k, j):
        q1, q2, q3 = roles(part)
        i1, i2, i3 = place(part)
        i3 = mod4(i3 + SHIFT[k])
        i2 = mod4(i2 - j)
        starts = []
        for i in range(4):
            cx, cy, cz = [
                (
                    same(q1, a) * i + same(q2, a) * i2 + same(q3, a) * i3) for a in range(3)]
            starts.append(pl.multiple_of(lax.div(cx, 2) * 4096 + cz * 1024 + lax.rem(cx, 2) * 512 + cy * 128, 128))
        weights = layer[part, i3, i2].reshape(8 * ROWS, COLS)

        @pl.loop(0, 1024 // TILE)
        def _(t):
            rows = pl.ds(pl.multiple_of(t * TILE, TILE), TILE)
            left = jnp.concatenate([tok[rows, pl.ds(s, 128)] for s in starts], axis=1)
            acc[part, rows, :] += jnp.dot(left, weights, preferred_element_type=F32)

    def same(q, a):
        if a == 0:
            return lax.div(2 - q, 2)
        return lax.rem(q, 2) if a == 1 else lax.div(q, 2)

    @pl.loop(0, PARTS)
    def _(part):
        columns = pl.ds(pl.multiple_of(part * COLS, COLS), COLS)

        @pl.loop(1, 8)
        def _(d):
            reduce_copy(part, d).wait_recv()

        averaged = pairs[part, chip].astype(F32)
        for d in range(7):
            averaged = averaged + landed[part, d].astype(F32)
        momentum_new = MOMENTUM_KEEP * mom[:, columns] + averaged
        master_new = mas[:, columns] - OUTER_RATE * (averaged + MOMENTUM_KEEP * momentum_new)
        mom[:, columns] = momentum_new
        mas[:, columns] = master_new
        i1, i2, i3 = place(part)
        layer[part, i3, i2, i1, core] = (gain_col * master_new).astype(BF16)
        for d in (1, 3, 2):
            line_send(part, d).start()

    mas_back = local_copy(mas, master_out, 4)
    mom_back = local_copy(mom, momentum_out, 5)
    mas_back.start()
    mom_back.start()

    @pl.loop(0, PARTS)
    def _(part):
        for d in (1, 3, 2):
            line_recv(part, d).wait_recv()
        for d in (1, 3, 2):
            plane_send(part, d).start()
        cube_send(part, 0, 0).start()
        cube_send(part, 1, 0).start()
        sibling_send(part, 0, 0).start()

    @pl.loop(1, 4)
    def _(d):
        @pl.loop(0, PARTS)
        def _(part):
            plane_recv(part, d).wait_recv()
            cube_send(part, 0, d).start()
            cube_send(part, 1, d).start()
            sibling_send(part, 0, d).start()
            sibling_recv(part, 0, d - 1).wait_recv()
            multiply(part, 0, d - 1)

    @pl.loop(0, 4)
    def _(j):
        @pl.loop(0, PARTS)
        def _(part):
            for way in (0, 1):
                cube_recv(part, way, j).wait_recv()
                sibling_send(part, 1 + way, j).start()

            @pl.when(lax.rem(j, 2) == 0)
            def _():
                forward_send(part, 0, j).start()

            @pl.when(lax.rem(j, 2) == 1)
            def _():
                forward_send(part, 1, j).start()

            @pl.when(j == 0)
            def _():
                sibling_recv(part, 0, 3).wait_recv()
                multiply(part, 0, 3)

            @pl.when(j > 0)
            def _():
                for k in (1, 2):
                    sibling_recv(part, k, j - 1).wait_recv()
                    multiply(part, k, j - 1)

    @pl.loop(0, 4)
    def _(j):
        @pl.loop(0, PARTS)
        def _(part):
            forward_recv(part, j).wait_recv()
            sibling_send(part, 3, j).start()

            @pl.when(j == 0)
            def _():
                for k in (1, 2):
                    sibling_recv(part, k, 3).wait_recv()
                    multiply(part, k, 3)

            @pl.when(j > 0)
            def _():
                sibling_recv(part, 3, j - 1).wait_recv()
                multiply(part, 3, j - 1)

    @pl.loop(0, PARTS)
    def _(part):
        sibling_recv(part, 3, 3).wait_recv()
        multiply(part, 3, 3)

    def keys_copy(t):
        rows = pl.ds(pl.multiple_of(t * TILE, TILE), TILE)
        return pltpu.make_async_copy(out.at[rows], keys.at[rows], local.at[6 + t])

    @pl.loop(0, 1024 // TILE)
    def _(t):
        rows = pl.ds(pl.multiple_of(t * TILE, TILE), TILE)
        scale = inv[rows, :][:, :1]
        for p in range(PARTS):
            out[rows, p * COLS:(p + 1) * COLS] = (acc[p, rows, :] * scale).astype(BF16)
        keys_copy(t).start()

    @pl.loop(0, PARTS)
    def _(part):
        @pl.loop(1, 8)
        def _(d):
            reduce_copy(part, d).wait_send()

        @pl.loop(1, 4)
        def _(d):
            line_send(part, d).wait_send()
            plane_send(part, d).wait_send()

        @pl.loop(0, 4)
        def _(j):
            cube_send(part, 0, j).wait_send()
            cube_send(part, 1, j).wait_send()
            forward_send(part, 0, j).wait_send()
            for k in range(4):
                sibling_send(part, k, j).wait_send()

    mas_back.wait()
    mom_back.wait()

    @pl.loop(0, 1024 // TILE)
    def _(t):
        keys_copy(t).wait()


def on_device(tokens, norm_gain, deltas, inner_steps, bucket_of_row, master, momentum):
    hbm = pl.BlockSpec(memory_space=pl.ANY)
    dma = pltpu.SemaphoreType.DMA
    return pl.pallas_call(
        kernel,
        out_shape=(
            jax.ShapeDtypeStruct((1024, 1024), BF16),
            jax.ShapeDtypeStruct((ROWS, 1024), F32),
            jax.ShapeDtypeStruct((ROWS, 1024), F32),
        ),
        in_specs=[hbm] * 7,
        out_specs=(hbm, hbm, hbm),
        scratch_shapes=[
            pltpu.VMEM((1024, 8192), BF16),
            pltpu.VMEM((PARTS, 4, 4, 4, 2, ROWS, COLS), BF16),
            pltpu.VMEM((PARTS, 1024, COLS), F32),
            pltpu.VMEM((8, ROWS, 1024), BF16),
            pltpu.VMEM((8, ROWS, 1024), BF16),
            pltpu.VMEM((PARTS, 8, ROWS, COLS), BF16),
            pltpu.VMEM((PARTS, 7, ROWS, COLS), BF16),
            pltpu.VMEM((ROWS, 1024), F32),
            pltpu.VMEM((ROWS, 1024), F32),
            pltpu.VMEM((64, 128), F32),
            pltpu.VMEM((16, 16), jnp.int32),
            pltpu.VMEM((8, 128), jnp.int32),
            pltpu.VMEM((2, 8, ROWS, 128), F32),
            pltpu.VMEM((1024, 128), F32),
            pltpu.VMEM((1024, 1024), BF16),
            dma((10,)),
            dma((2,)),
            dma((PARTS, 7)),
            dma((PARTS, 7)),
            dma((PARTS, COPIES)),
            dma((PARTS, COPIES)),
        ],
        compiler_params=pltpu.CompilerParams(
            collective_id=0, has_side_effects=True, vmem_limit_bytes=56 * 1024 * 1024),
        cost_estimate=pl.CostEstimate(flops=2 * 1024 * 8192 * 1024, bytes_accessed=24 << 20, transcendentals=1024),
    )(
        tokens,
        norm_gain.astype(F32).reshape(64, 128),
        deltas.reshape(8, 2, ROWS, 1024),
        inner_steps,
        bucket_of_row.reshape(8, 128),
        master,
        momentum,
    )


def solution(mesh):
    in_specs = (
        P(("rep", "fsdp"), None),
        P(),
        P("rep", "fsdp", None),
        P(),
        P("fsdp"),
        P(("fsdp", "rep"), None),
        P(("fsdp", "rep"), None),
    )
    out_specs = (P(("rep", "fsdp"), None), P(("fsdp", "rep"), None), P(("fsdp", "rep"), None))
    return jax.shard_map(
        on_device, mesh=mesh, in_specs=in_specs, out_specs=out_specs, check_vma=False
    )
```

```python
import jax
import jax.numpy as jnp
from jax import lax
from jax.experimental import pallas as pl
from jax.experimental.pallas import tpu as pltpu
from jax.sharding import PartitionSpec as P

OUTER_RATE = 0.7
MOMENTUM_KEEP = 0.9
EPSILON = 1e-05
MESH = pl.DeviceIdType.MESH
F32 = jnp.float32
BF16 = jnp.bfloat16

SPANS = ((0, 384), (384, 384), (768, 256))
PARTS = range(3)
ROWS = 64
TILE = 256
LINE, PLANE, CUBE, FORWARD, SIBLING, COPIES = 0, 3, 6, 14, 18, 34
ITEMS = 16


def mod4(v):
    return lax.rem(v + 8, 4)


def position():
    rep = lax.axis_index("rep")
    fsdp = lax.axis_index("fsdp")
    x = lax.div(fsdp, 4) * 2 + lax.div(rep, 8)
    y = lax.rem(lax.div(rep, 2), 4)
    z = lax.rem(fsdp, 4)
    return x, y, z, lax.rem(rep, 2)


def device(x, y, z, core):
    return (lax.rem(x, 2) * 8 + y * 2 + core, lax.div(x, 2) * 4 + z)


def roles(part):
    return part % 3, (part + 1) % 3, (part + 2) % 3


def item_place(m):
    group = lax.div(m, 4)
    first, last = lax.div(3 - group, 3), lax.div(group, 3)
    middle = 1 - first - last
    shift = middle * (2 * lax.rem(m, 2) - 1) + 2 * last
    return shift, (first + last) * lax.rem(m, 4) + middle * (lax.div(m, 2) - 2)


def kernel(tokens, gain, deltas, steps, bucket, master, momentum,
           keys, master_out, momentum_out,
           tok, layer0, layer1, layer2, acc0, acc1, acc2, own, sib, pairs, landed, mas, mom, gain_v, steps_v, bucket_v,
           wcol, inv, out, local, pair_s, pair_r, red_s, red_r, gat_s, gat_r):
    layer = (layer0, layer1, layer2)
    acc = (acc0, acc1, acc2)
    here = position()
    x, y, z, core = here
    chip = lax.rem(x, 2) * 4 + y
    sibling = device(x, y, z, 1 - core)

    def columns(part):
        return pl.ds(*SPANS[part])

    def local_copy(src, dst, i):
        return pltpu.make_async_copy(src, dst, local.at[i])

    steps_copy = local_copy(steps, steps_v, 0)
    bucket_copy = local_copy(bucket, bucket_v, 1)
    gain_copy = local_copy(
        gain.at[pl.ds(pl.multiple_of(lax.axis_index("fsdp") * 1024, 1024), 1024)], gain_v, 2)
    mas_copy = local_copy(master, mas, 3)
    mom_copy = local_copy(momentum, mom, 4)
    own_copies = [local_copy(deltas.at[:, core, :, columns(p)], own.at[:, :, columns(p)], 5 + p) for p in PARTS]
    tok_copies = [
        local_copy(tokens.at[pl.ds(i * TILE, TILE)], tok.at[pl.ds(i * TILE, TILE)], 8 + i) for i in range(4)]
    for copy in [steps_copy, bucket_copy] + own_copies + [gain_copy, mas_copy, mom_copy] + tok_copies:
        copy.start()

    barrier = pltpu.get_barrier_semaphore()
    peers = [sibling]
    for d in range(1, 8):
        k = lax.rem(chip + d, 8)
        peers.append(device(lax.div(x, 2) * 2 + lax.div(k, 4), lax.rem(k, 4), z, core))
    far = (1 - lax.div(x, 2)) * 2
    peers.append(device(far, y, z, core))
    peers.append(device(far + 1, y, z, core))
    for d in range(1, 4):
        peers.append(device(x, y, mod4(z + d), core))
    for peer in peers:
        pl.semaphore_signal(barrier, inc=1, device_id=peer, device_id_type=MESH)
    pl.semaphore_wait(barrier, len(peers))

    pair_copies = [
        pltpu.make_async_remote_copy(
            src_ref=deltas.at[:, 1 - core, :, columns(p)], dst_ref=sib.at[:, :, columns(p)],
            send_sem=pair_s.at[p], recv_sem=pair_r.at[p], device_id=sibling, device_id_type=MESH)
        for p in PARTS]
    for copy in pair_copies:
        copy.start()

    steps_copy.wait()
    bucket_copy.wait()
    counts = steps_v[...].astype(F32)
    share = counts / jnp.sum(counts, axis=0, keepdims=True)
    replica = lax.axis_index("rep")
    replica_ids = lax.broadcasted_iota(jnp.int32, (16, 16), 0)
    lane = lax.broadcasted_iota(jnp.int32, (ROWS, 128), 1)
    row = lax.broadcasted_iota(jnp.int32, (ROWS, 128), 0)
    mine = lane == row + core * ROWS
    buckets = bucket_v[...]
    for side, who in enumerate((replica, replica + 1 - 2 * core)):
        row_share = jnp.sum(jnp.where(replica_ids == who, share, 0.0), axis=0, keepdims=True)
        weight = jnp.zeros((8, 128), F32)
        for b in range(16):
            weight = weight + jnp.where(buckets == b, row_share[:, b:b + 1], 0.0)
        for k in range(8):
            column = jnp.sum(jnp.where(mine, weight[k:k + 1, :], 0.0), axis=1, keepdims=True)
            wcol[side, k] = jnp.broadcast_to(column, (ROWS, 128))

    def reduce_copy(part, d):
        k = lax.rem(chip + d, 8)
        return pltpu.make_async_remote_copy(
            src_ref=pairs.at[k, :, columns(part)], dst_ref=landed.at[d - 1, :, columns(part)],
            send_sem=red_s.at[part, d - 1], recv_sem=red_r.at[part, d - 1],
            device_id=device(lax.div(x, 2) * 2 + lax.div(k, 4), lax.rem(k, 4), z, core), device_id_type=MESH)

    for p in PARTS:
        own_copies[p].wait()
        pair_copies[p].wait_recv()

        @pl.loop(0, 8)
        def _(k):
            w0 = wcol[0, k][:, :1]
            w1 = wcol[1, k][:, :1]
            both = w0 * own[k, :, columns(p)].astype(F32) + w1 * sib[k, :, columns(p)].astype(F32)
            pairs[k, :, columns(p)] = both.astype(BF16)

        @pl.loop(1, 8)
        def _(d):
            reduce_copy(p, d).start()

    for ref in acc:
        ref[...] = jnp.zeros_like(ref)
    gain_copy.wait()
    gain_rows = gain_v[...].astype(F32).reshape(8, 128)
    gain_row = jnp.sum(
        jnp.where(lax.broadcasted_iota(jnp.int32, (8, 128), 0) == chip, gain_rows, 0.0), axis=0, keepdims=True)
    gain_col = jnp.sum(jnp.where(mine, gain_row, 0.0), axis=1, keepdims=True)
    mas_copy.wait()
    mom_copy.wait()
    for copy in tok_copies:
        copy.wait()

    @pl.loop(0, 1024 // 32)
    def _(i):
        rows = pl.ds(pl.multiple_of(i * 32, 32), 32)
        total = jnp.zeros((32, 128), F32)
        for j in range(64):
            v = tok[rows, j * 128:(j + 1) * 128].astype(F32)
            total = total + v * v
        mean = jnp.sum(total, axis=1, keepdims=True) * (1.0 / 8192.0)
        inv[rows, :] = jnp.broadcast_to(lax.rsqrt(mean + EPSILON), (32, 128))

    def place(part):
        return [here[q] for q in roles(part)]

    def along(axis, d):
        moved = [mod4(v + d) if q == axis else v for q, v in enumerate((x, y, z))]
        return device(*moved, core)

    def gather_copy(part, ref, index, target):
        return pltpu.make_async_remote_copy(
            src_ref=ref, dst_ref=ref, send_sem=gat_s.at[part, index], recv_sem=gat_r.at[part, index],
            device_id=target, device_id_type=MESH)

    def line_send(part, d):
        i1, i2, i3 = place(part)
        return gather_copy(part, layer[part].at[i3, i2, i1, core], LINE + d - 1, along(roles(part)[0], d))

    def line_recv(part, d):
        i1, i2, i3 = place(part)
        return gather_copy(part, layer[part].at[i3, i2, mod4(i1 - d), core], LINE + d - 1, sibling)

    def a_line(part, m, who):
        shift, j = item_place(m)
        i1, i2, i3 = place(part)
        return layer[part].at[mod4(i3 + shift), mod4(i2 - j), :, who]

    def plane_send(part, d):
        return gather_copy(part, a_line(part, 0, core), PLANE + d - 1, along(roles(part)[1], d))

    def plane_recv(part, d):
        return gather_copy(part, a_line(part, d, core), PLANE + d - 1, sibling)

    def cube_send(part, way, j):
        return gather_copy(part, a_line(part, j, core), CUBE + 2 * j + way, along(roles(part)[2], 1 - 2 * way))

    def cube_recv(part, m):
        return gather_copy(part, a_line(part, m, core), CUBE + m - 4, sibling)

    def forward_send(part, m):
        way = lax.rem(m, 2)
        return gather_copy(
            part, a_line(part, m, core), FORWARD + lax.div(m, 2) - 2, along(roles(part)[2], 1 - 2 * way))

    def forward_recv(part, m):
        return gather_copy(part, a_line(part, m, core), FORWARD + m - 12, sibling)

    def sibling_send(part, m):
        return gather_copy(part, a_line(part, m, core), SIBLING + m, sibling)

    def sibling_recv(part, m):
        return gather_copy(part, a_line(part, m, 1 - core), SIBLING + m, sibling)

    def multiply(part, m):
        q1, q2, q3 = roles(part)
        i1, i2, i3 = place(part)
        shift, j = item_place(m)
        spot = [None, None, None]
        spot[q2] = mod4(i2 - j)
        spot[q3] = mod4(i3 + shift)
        weights = layer[part][spot[q3], spot[q2]].reshape(8 * ROWS, SPANS[part][1])
        left = []
        for i in range(4):
            spot[q1] = i
            start = lax.div(spot[0], 2) * 4096 + spot[2] * 1024 + lax.rem(spot[0], 2) * 512 + spot[1] * 128
            left.append(tok[:, pl.ds(pl.multiple_of(start, 128), 128)])
        acc[part][...] += jnp.dot(jnp.concatenate(left, axis=1), weights, preferred_element_type=F32)

    for p in PARTS:
        @pl.loop(1, 8)
        def _(d):
            reduce_copy(p, d).wait_recv()

        averaged = pairs[chip, :, columns(p)].astype(F32)
        for d in range(7):
            averaged = averaged + landed[d, :, columns(p)].astype(F32)
        momentum_new = MOMENTUM_KEEP * mom[:, columns(p)] + averaged
        master_new = mas[:, columns(p)] - OUTER_RATE * (averaged + MOMENTUM_KEEP * momentum_new)
        mom[:, columns(p)] = momentum_new
        mas[:, columns(p)] = master_new
        i1, i2, i3 = place(p)
        layer[p][i3, i2, i1, core] = (gain_col * master_new).astype(BF16)
        for d in (1, 3, 2):
            line_send(p, d).start()

    mas_back = local_copy(mas, master_out, 3)
    mom_back = local_copy(mom, momentum_out, 4)
    mas_back.start()
    mom_back.start()

    @pl.loop(0, ITEMS + 1)
    def _(m):
        for p in PARTS:
            @pl.when(m == 0)
            def _():
                for d in (1, 3, 2):
                    line_recv(p, d).wait_recv()
                for d in (1, 3, 2):
                    plane_send(p, d).start()

            @pl.when((m >= 1) & (m < 4))
            def _():
                plane_recv(p, m).wait_recv()

            @pl.when(m < 4)
            def _():
                cube_send(p, 0, m).start()
                cube_send(p, 1, m).start()

            @pl.when((m >= 4) & (m < 12))
            def _():
                cube_recv(p, m).wait_recv()

                @pl.when(lax.rem(lax.div(m, 2), 2) == lax.rem(m, 2))
                def _():
                    forward_send(p, m).start()

            @pl.when((m >= 12) & (m < ITEMS))
            def _():
                forward_recv(p, m).wait_recv()

            @pl.when(m < ITEMS)
            def _():
                sibling_send(p, m).start()

            @pl.when(m >= 1)
            def _():
                sibling_recv(p, m - 1).wait_recv()
                multiply(p, m - 1)

    def keys_copy(t):
        rows = pl.ds(pl.multiple_of(t * TILE, TILE), TILE)
        return pltpu.make_async_copy(out.at[rows], keys.at[rows], local.at[8 + t])

    @pl.loop(0, 1024 // TILE)
    def _(t):
        rows = pl.ds(pl.multiple_of(t * TILE, TILE), TILE)
        scale = inv[rows, :][:, :1]
        for p in PARTS:
            out[rows, columns(p)] = (acc[p][rows, :] * scale).astype(BF16)
        keys_copy(t).start()

    for p in PARTS:
        pair_copies[p].wait_send()

        @pl.loop(1, 8)
        def _(d):
            reduce_copy(p, d).wait_send()

        @pl.loop(1, 4)
        def _(d):
            line_send(p, d).wait_send()
            plane_send(p, d).wait_send()

        @pl.loop(0, 4)
        def _(j):
            cube_send(p, 0, j).wait_send()
            cube_send(p, 1, j).wait_send()
            forward_send(p, 2 * j + 4).wait_send()

        @pl.loop(0, ITEMS)
        def _(m):
            sibling_send(p, m).wait_send()

    mas_back.wait()
    mom_back.wait()

    @pl.loop(0, 1024 // TILE)
    def _(t):
        keys_copy(t).wait()


def on_device(tokens, norm_gain, deltas, inner_steps, bucket_of_row, master, momentum):
    hbm = pl.BlockSpec(memory_space=pl.ANY)
    dma = pltpu.SemaphoreType.DMA
    return pl.pallas_call(
        kernel,
        out_shape=(
            jax.ShapeDtypeStruct((1024, 1024), BF16),
            jax.ShapeDtypeStruct((ROWS, 1024), F32),
            jax.ShapeDtypeStruct((ROWS, 1024), F32),
        ),
        in_specs=[hbm] * 7,
        out_specs=(hbm, hbm, hbm),
        scratch_shapes=[
            pltpu.VMEM((1024, 8192), BF16),
            *[pltpu.VMEM((4, 4, 4, 2, ROWS, width), BF16) for _, width in SPANS],
            *[pltpu.VMEM((1024, width), F32) for _, width in SPANS],
            pltpu.VMEM((8, ROWS, 1024), BF16),
            pltpu.VMEM((8, ROWS, 1024), BF16),
            pltpu.VMEM((8, ROWS, 1024), BF16),
            pltpu.VMEM((7, ROWS, 1024), BF16),
            pltpu.VMEM((ROWS, 1024), F32),
            pltpu.VMEM((ROWS, 1024), F32),
            pltpu.VMEM((1024,), BF16),
            pltpu.VMEM((16, 16), jnp.int32),
            pltpu.VMEM((8, 128), jnp.int32),
            pltpu.VMEM((2, 8, ROWS, 128), F32),
            pltpu.VMEM((1024, 128), F32),
            pltpu.VMEM((1024, 1024), BF16),
            dma((12,)),
            dma((3,)),
            dma((3,)),
            dma((3, 7)),
            dma((3, 7)),
            dma((3, COPIES)),
            dma((3, COPIES)),
        ],
        compiler_params=pltpu.CompilerParams(
            collective_id=0, has_side_effects=True, vmem_limit_bytes=56 * 1024 * 1024),
        cost_estimate=pl.CostEstimate(flops=2 * 1024 * 8192 * 1024, bytes_accessed=24 << 20, transcendentals=1024),
    )(
        tokens,
        norm_gain,
        deltas.reshape(8, 2, ROWS, 1024),
        inner_steps,
        bucket_of_row.reshape(8, 128),
        master,
        momentum,
    )


def solution(mesh):
    in_specs = (
        P(("rep", "fsdp"), None),
        P(),
        P("rep", "fsdp", None),
        P(),
        P("fsdp"),
        P(("fsdp", "rep"), None),
        P(("fsdp", "rep"), None),
    )
    out_specs = (P(("rep", "fsdp"), None), P(("fsdp", "rep"), None), P(("fsdp", "rep"), None))
    return jax.shard_map(
        on_device, mesh=mesh, in_specs=in_specs, out_specs=out_specs, check_vma=False
    )
```

```python
import jax
import jax.numpy as jnp
from jax import lax
from jax.experimental import pallas as pl
from jax.experimental.pallas import tpu as pltpu
from jax.sharding import PartitionSpec as P

OUTER_RATE = 0.7
MOMENTUM_KEEP = 0.9
EPSILON = 1e-05
MESH = pl.DeviceIdType.MESH
F32 = jnp.float32
BF16 = jnp.bfloat16

SPANS = ((0, 384), (384, 384), (768, 256))
ORDERS = ((1, 0, 2), (2, 1, 0), (0, 2, 1))
PARTS = range(3)
ROWS = 64
TILE = 256
LINE, PLANE, CUBE, FORWARD, SIBLING, COPIES = 0, 3, 6, 14, 18, 34
ITEMS = 16


def mod4(v):
    return lax.rem(v + 8, 4)


def position():
    rep = lax.axis_index("rep")
    fsdp = lax.axis_index("fsdp")
    x = lax.div(fsdp, 4) * 2 + lax.div(rep, 8)
    y = lax.rem(lax.div(rep, 2), 4)
    z = lax.rem(fsdp, 4)
    return x, y, z, lax.rem(rep, 2)


def device(x, y, z, core):
    return (lax.rem(x, 2) * 8 + y * 2 + core, lax.div(x, 2) * 4 + z)


def roles(part):
    return ORDERS[part]


def item_place(m):
    group = lax.div(m, 4)
    first, last = lax.div(3 - group, 3), lax.div(group, 3)
    middle = 1 - first - last
    shift = middle * (2 * lax.rem(m, 2) - 1) + 2 * last
    return shift, (first + last) * lax.rem(m, 4) + middle * (lax.div(m, 2) - 2)


def kernel(tokens, gain, deltas, steps, bucket, master, momentum,
           keys, master_out, momentum_out,
           tok, layer0, layer1, layer2, acc0, acc1, acc2, own, sib, pairs, landed, mas, mom, gain_v, steps_v, bucket_v,
           wcol, inv, out, local, pair_s, pair_r, red_s, red_r, gat_s, gat_r):
    layer = (layer0, layer1, layer2)
    acc = (acc0, acc1, acc2)
    here = position()
    x, y, z, core = here
    chip = lax.rem(x, 2) * 4 + y
    sibling = device(x, y, z, 1 - core)

    def columns(part):
        return pl.ds(*SPANS[part])

    def local_copy(src, dst, i):
        return pltpu.make_async_copy(src, dst, local.at[i])

    steps_copy = local_copy(steps, steps_v, 0)
    bucket_copy = local_copy(bucket, bucket_v, 1)
    gain_copy = local_copy(
        gain.at[pl.ds(pl.multiple_of(lax.axis_index("fsdp") * 1024, 1024), 1024)], gain_v, 2)
    mas_copy = local_copy(master, mas, 3)
    mom_copy = local_copy(momentum, mom, 4)
    own_copies = [local_copy(deltas.at[:, core, :, columns(p)], own.at[:, :, columns(p)], 5 + p) for p in PARTS]
    tok_copies = [
        local_copy(tokens.at[pl.ds(i * TILE, TILE)], tok.at[pl.ds(i * TILE, TILE)], 8 + i) for i in range(4)]
    for copy in [steps_copy, bucket_copy] + own_copies + [gain_copy, mas_copy, mom_copy] + tok_copies:
        copy.start()

    barrier = pltpu.get_barrier_semaphore()
    peers = [sibling]
    for d in range(1, 8):
        k = lax.rem(chip + d, 8)
        peers.append(device(lax.div(x, 2) * 2 + lax.div(k, 4), lax.rem(k, 4), z, core))
    far = (1 - lax.div(x, 2)) * 2
    peers.append(device(far, y, z, core))
    peers.append(device(far + 1, y, z, core))
    for d in range(1, 4):
        peers.append(device(x, y, mod4(z + d), core))
    for peer in peers:
        pl.semaphore_signal(barrier, inc=1, device_id=peer, device_id_type=MESH)
    pl.semaphore_wait(barrier, len(peers))

    pair_copies = [
        pltpu.make_async_remote_copy(
            src_ref=deltas.at[:, 1 - core, :, columns(p)], dst_ref=sib.at[:, :, columns(p)],
            send_sem=pair_s.at[p], recv_sem=pair_r.at[p], device_id=sibling, device_id_type=MESH)
        for p in PARTS]
    for copy in pair_copies:
        copy.start()

    steps_copy.wait()
    bucket_copy.wait()
    counts = steps_v[...].astype(F32)
    share = counts / jnp.sum(counts, axis=0, keepdims=True)
    replica = lax.axis_index("rep")
    replica_ids = lax.broadcasted_iota(jnp.int32, (16, 16), 0)
    lane = lax.broadcasted_iota(jnp.int32, (ROWS, 128), 1)
    row = lax.broadcasted_iota(jnp.int32, (ROWS, 128), 0)
    mine = lane == row + core * ROWS
    buckets = bucket_v[...]
    for side, who in enumerate((replica, replica + 1 - 2 * core)):
        row_share = jnp.sum(jnp.where(replica_ids == who, share, 0.0), axis=0, keepdims=True)
        weight = jnp.zeros((8, 128), F32)
        for b in range(16):
            weight = weight + jnp.where(buckets == b, row_share[:, b:b + 1], 0.0)
        for k in range(8):
            column = jnp.sum(jnp.where(mine, weight[k:k + 1, :], 0.0), axis=1, keepdims=True)
            wcol[side, k] = jnp.broadcast_to(column, (ROWS, 128))

    def reduce_copy(part, d):
        k = lax.rem(chip + d, 8)
        return pltpu.make_async_remote_copy(
            src_ref=pairs.at[k, :, columns(part)], dst_ref=landed.at[d - 1, :, columns(part)],
            send_sem=red_s.at[part, d - 1], recv_sem=red_r.at[part, d - 1],
            device_id=device(lax.div(x, 2) * 2 + lax.div(k, 4), lax.rem(k, 4), z, core), device_id_type=MESH)

    for p in PARTS:
        own_copies[p].wait()
        pair_copies[p].wait_recv()

        @pl.loop(0, 8)
        def _(k):
            w0 = wcol[0, k][:, :1]
            w1 = wcol[1, k][:, :1]
            both = w0 * own[k, :, columns(p)].astype(F32) + w1 * sib[k, :, columns(p)].astype(F32)
            pairs[k, :, columns(p)] = both.astype(BF16)

        @pl.loop(1, 8)
        def _(d):
            reduce_copy(p, d).start()

    for ref in acc:
        ref[...] = jnp.zeros_like(ref)
    gain_copy.wait()
    gain_rows = gain_v[...].astype(F32).reshape(8, 128)
    gain_row = jnp.sum(
        jnp.where(lax.broadcasted_iota(jnp.int32, (8, 128), 0) == chip, gain_rows, 0.0), axis=0, keepdims=True)
    gain_col = jnp.sum(jnp.where(mine, gain_row, 0.0), axis=1, keepdims=True)
    mas_copy.wait()
    mom_copy.wait()
    for copy in tok_copies:
        copy.wait()

    @pl.loop(0, 1024 // 32)
    def _(i):
        rows = pl.ds(pl.multiple_of(i * 32, 32), 32)
        total = jnp.zeros((32, 128), F32)
        for j in range(64):
            v = tok[rows, j * 128:(j + 1) * 128].astype(F32)
            total = total + v * v
        mean = jnp.sum(total, axis=1, keepdims=True) * (1.0 / 8192.0)
        inv[rows, :] = jnp.broadcast_to(lax.rsqrt(mean + EPSILON), (32, 128))

    def place(part):
        return [here[q] for q in roles(part)]

    def along(axis, d):
        moved = [mod4(v + d) if q == axis else v for q, v in enumerate((x, y, z))]
        return device(*moved, core)

    def gather_copy(part, ref, index, target):
        return pltpu.make_async_remote_copy(
            src_ref=ref, dst_ref=ref, send_sem=gat_s.at[part, index], recv_sem=gat_r.at[part, index],
            device_id=target, device_id_type=MESH)

    def line_send(part, d):
        i1, i2, i3 = place(part)
        return gather_copy(part, layer[part].at[i3, i2, i1, core], LINE + d - 1, along(roles(part)[0], d))

    def line_recv(part, d):
        i1, i2, i3 = place(part)
        return gather_copy(part, layer[part].at[i3, i2, mod4(i1 - d), core], LINE + d - 1, sibling)

    def a_line(part, m, who):
        shift, j = item_place(m)
        i1, i2, i3 = place(part)
        return layer[part].at[mod4(i3 + shift), mod4(i2 - j), :, who]

    def plane_send(part, d):
        return gather_copy(part, a_line(part, 0, core), PLANE + d - 1, along(roles(part)[1], d))

    def plane_recv(part, d):
        return gather_copy(part, a_line(part, d, core), PLANE + d - 1, sibling)

    def cube_send(part, way, j):
        return gather_copy(part, a_line(part, j, core), CUBE + 2 * j + way, along(roles(part)[2], 1 - 2 * way))

    def cube_recv(part, m):
        return gather_copy(part, a_line(part, m, core), CUBE + m - 4, sibling)

    def forward_send(part, m):
        way = lax.rem(m, 2)
        return gather_copy(
            part, a_line(part, m, core), FORWARD + lax.div(m, 2) - 2, along(roles(part)[2], 1 - 2 * way))

    def forward_recv(part, m):
        return gather_copy(part, a_line(part, m, core), FORWARD + m - 12, sibling)

    def sibling_send(part, m):
        return gather_copy(part, a_line(part, m, core), SIBLING + m, sibling)

    def sibling_recv(part, m):
        return gather_copy(part, a_line(part, m, 1 - core), SIBLING + m, sibling)

    def multiply(part, m):
        q1, q2, q3 = roles(part)
        i1, i2, i3 = place(part)
        shift, j = item_place(m)
        spot = [None, None, None]
        spot[q2] = mod4(i2 - j)
        spot[q3] = mod4(i3 + shift)
        weights = layer[part][spot[q3], spot[q2]].reshape(8 * ROWS, SPANS[part][1])
        left = []
        for i in range(4):
            spot[q1] = i
            start = lax.div(spot[0], 2) * 4096 + spot[2] * 1024 + lax.rem(spot[0], 2) * 512 + spot[1] * 128
            left.append(tok[:, pl.ds(pl.multiple_of(start, 128), 128)])
        acc[part][...] += jnp.dot(jnp.concatenate(left, axis=1), weights, preferred_element_type=F32)

    for p in PARTS:
        @pl.loop(1, 8)
        def _(d):
            reduce_copy(p, d).wait_recv()

        averaged = pairs[chip, :, columns(p)].astype(F32)
        for d in range(7):
            averaged = averaged + landed[d, :, columns(p)].astype(F32)
        momentum_new = MOMENTUM_KEEP * mom[:, columns(p)] + averaged
        master_new = mas[:, columns(p)] - OUTER_RATE * (averaged + MOMENTUM_KEEP * momentum_new)
        mom[:, columns(p)] = momentum_new
        mas[:, columns(p)] = master_new
        i1, i2, i3 = place(p)
        layer[p][i3, i2, i1, core] = (gain_col * master_new).astype(BF16)
        for d in (1, 3, 2):
            line_send(p, d).start()

    mas_back = local_copy(mas, master_out, 3)
    mom_back = local_copy(mom, momentum_out, 4)
    mas_back.start()
    mom_back.start()

    @pl.loop(0, ITEMS + 1)
    def _(m):
        for p in PARTS:
            @pl.when(m == 0)
            def _():
                for d in (1, 3, 2):
                    line_recv(p, d).wait_recv()
                for d in (1, 3, 2):
                    plane_send(p, d).start()

            @pl.when((m >= 1) & (m < 4))
            def _():
                plane_recv(p, m).wait_recv()

            @pl.when(m < 4)
            def _():
                cube_send(p, 0, m).start()
                cube_send(p, 1, m).start()

            @pl.when((m >= 4) & (m < 12))
            def _():
                cube_recv(p, m).wait_recv()

                @pl.when(lax.rem(lax.div(m, 2), 2) == lax.rem(m, 2))
                def _():
                    forward_send(p, m).start()

            @pl.when((m >= 12) & (m < ITEMS))
            def _():
                forward_recv(p, m).wait_recv()

            @pl.when(m < ITEMS)
            def _():
                sibling_send(p, m).start()

            @pl.when(m >= 1)
            def _():
                sibling_recv(p, m - 1).wait_recv()
                multiply(p, m - 1)

    def keys_copy(t):
        rows = pl.ds(pl.multiple_of(t * TILE, TILE), TILE)
        return pltpu.make_async_copy(out.at[rows], keys.at[rows], local.at[8 + t])

    @pl.loop(0, 1024 // TILE)
    def _(t):
        rows = pl.ds(pl.multiple_of(t * TILE, TILE), TILE)
        scale = inv[rows, :][:, :1]
        for p in PARTS:
            out[rows, columns(p)] = (acc[p][rows, :] * scale).astype(BF16)
        keys_copy(t).start()

    for p in PARTS:
        pair_copies[p].wait_send()

        @pl.loop(1, 8)
        def _(d):
            reduce_copy(p, d).wait_send()

        @pl.loop(1, 4)
        def _(d):
            line_send(p, d).wait_send()
            plane_send(p, d).wait_send()

        @pl.loop(0, 4)
        def _(j):
            cube_send(p, 0, j).wait_send()
            cube_send(p, 1, j).wait_send()
            forward_send(p, 2 * j + 4).wait_send()

        @pl.loop(0, ITEMS)
        def _(m):
            sibling_send(p, m).wait_send()

    mas_back.wait()
    mom_back.wait()

    @pl.loop(0, 1024 // TILE)
    def _(t):
        keys_copy(t).wait()


def relay(keys, master_new, momentum_new, keys_out, master_out, momentum_out, keys_v, mas_v, mom_v, into, done):
    spans = [pl.ds(i * TILE, TILE) for i in range(4)]
    hops = [(keys.at[s], keys_v.at[s], keys_out.at[s]) for s in spans]
    hops += [(master_new, mas_v, master_out), (momentum_new, mom_v, momentum_out)]
    reads = [pltpu.make_async_copy(a, b, into.at[i]) for i, (a, b, _) in enumerate(hops)]
    writes = [pltpu.make_async_copy(b, c, done.at[i]) for i, (_, b, c) in enumerate(hops)]
    for copy in reads:
        copy.start()
    for read, write in zip(reads, writes):
        read.wait()
        write.start()
    for copy in writes:
        copy.wait()


def on_device(tokens, norm_gain, deltas, inner_steps, bucket_of_row, master, momentum):
    hbm = pl.BlockSpec(memory_space=pl.ANY)
    dma = pltpu.SemaphoreType.DMA
    shapes = (
        jax.ShapeDtypeStruct((1024, 1024), BF16),
        jax.ShapeDtypeStruct((ROWS, 1024), F32),
        jax.ShapeDtypeStruct((ROWS, 1024), F32),
    )
    results = pl.pallas_call(
        kernel,
        out_shape=shapes,
        in_specs=[hbm] * 7,
        out_specs=(hbm, hbm, hbm),
        scratch_shapes=[
            pltpu.VMEM((1024, 8192), BF16),
            *[pltpu.VMEM((4, 4, 4, 2, ROWS, width), BF16) for _, width in SPANS],
            *[pltpu.VMEM((1024, width), F32) for _, width in SPANS],
            pltpu.VMEM((8, ROWS, 1024), BF16),
            pltpu.VMEM((8, ROWS, 1024), BF16),
            pltpu.VMEM((8, ROWS, 1024), BF16),
            pltpu.VMEM((7, ROWS, 1024), BF16),
            pltpu.VMEM((ROWS, 1024), F32),
            pltpu.VMEM((ROWS, 1024), F32),
            pltpu.VMEM((1024,), BF16),
            pltpu.VMEM((16, 16), jnp.int32),
            pltpu.VMEM((8, 128), jnp.int32),
            pltpu.VMEM((2, 8, ROWS, 128), F32),
            pltpu.VMEM((1024, 128), F32),
            pltpu.VMEM((1024, 1024), BF16),
            dma((12,)),
            dma((3,)),
            dma((3,)),
            dma((3, 7)),
            dma((3, 7)),
            dma((3, COPIES)),
            dma((3, COPIES)),
        ],
        compiler_params=pltpu.CompilerParams(
            collective_id=0, has_side_effects=True, vmem_limit_bytes=56 * 1024 * 1024),
        cost_estimate=pl.CostEstimate(flops=2 * 1024 * 8192 * 1024, bytes_accessed=24 << 20, transcendentals=1024),
    )(
        tokens,
        norm_gain,
        deltas.reshape(8, 2, ROWS, 1024),
        inner_steps,
        bucket_of_row.reshape(8, 128),
        master,
        momentum,
    )
    return pl.pallas_call(
        relay,
        out_shape=shapes,
        in_specs=[hbm] * 3,
        out_specs=(hbm, hbm, hbm),
        scratch_shapes=[pltpu.VMEM(s.shape, s.dtype) for s in shapes] + [dma((6,)), dma((6,))],
        compiler_params=pltpu.CompilerParams(vmem_limit_bytes=56 * 1024 * 1024),
    )(*results)


def solution(mesh):
    in_specs = (
        P(("rep", "fsdp"), None),
        P(),
        P("rep", "fsdp", None),
        P(),
        P("fsdp"),
        P(("fsdp", "rep"), None),
        P(("fsdp", "rep"), None),
    )
    out_specs = (P(("rep", "fsdp"), None), P(("fsdp", "rep"), None), P(("fsdp", "rep"), None))
    return jax.shard_map(
        on_device, mesh=mesh, in_specs=in_specs, out_specs=out_specs, check_vma=False
    )
```

```python
import jax
import jax.numpy as jnp
from jax import lax
from jax.experimental import pallas as pl
from jax.experimental.pallas import tpu as pltpu
from jax.sharding import PartitionSpec as P

OUTER_RATE = 0.7
MOMENTUM_KEEP = 0.9
EPSILON = 1e-05
MESH = pl.DeviceIdType.MESH
F32 = jnp.float32
BF16 = jnp.bfloat16

SPANS = ((0, 384), (384, 384), (768, 256))
ORDERS = ((1, 0, 2), (2, 1, 0), (0, 2, 1))
PARTS = range(3)
ROWS = 64
TILE = 256
LINE, PLANE, CUBE, FORWARD, SIBLING, COPIES = 0, 3, 6, 14, 18, 34
ITEMS = 16


def mod4(v):
    return lax.rem(v + 8, 4)


def position():
    rep = lax.axis_index("rep")
    fsdp = lax.axis_index("fsdp")
    x = lax.div(fsdp, 4) * 2 + lax.div(rep, 8)
    y = lax.rem(lax.div(rep, 2), 4)
    z = lax.rem(fsdp, 4)
    return x, y, z, lax.rem(rep, 2)


def device(x, y, z, core):
    return (lax.rem(x, 2) * 8 + y * 2 + core, lax.div(x, 2) * 4 + z)


def roles(part):
    return ORDERS[part]


def item_place(m):
    group = lax.div(m, 4)
    first, last = lax.div(3 - group, 3), lax.div(group, 3)
    middle = 1 - first - last
    shift = middle * (2 * lax.rem(m, 2) - 1) + 2 * last
    return shift, (first + last) * lax.rem(m, 4) + middle * (lax.div(m, 2) - 2)


def kernel(tokens, gain, deltas, steps, bucket, master, momentum,
           keys, master_out, momentum_out,
           tok, layer0, layer1, layer2, acc0, acc1, acc2, own, sib, pairs, landed, mas, mom, gain_v, steps_v, bucket_v,
           wcol, inv, out, local, pair_s, pair_r, red_s, red_r, gat_s, gat_r):
    layer = (layer0, layer1, layer2)
    acc = (acc0, acc1, acc2)
    here = position()
    x, y, z, core = here
    chip = lax.rem(x, 2) * 4 + y
    sibling = device(x, y, z, 1 - core)

    def columns(part):
        return pl.ds(*SPANS[part])

    def local_copy(src, dst, i):
        return pltpu.make_async_copy(src, dst, local.at[i])

    steps_copy = local_copy(steps, steps_v, 0)
    bucket_copy = local_copy(bucket, bucket_v, 1)
    gain_copy = local_copy(
        gain.at[pl.ds(pl.multiple_of(lax.axis_index("fsdp") * 1024, 1024), 1024)], gain_v, 2)
    mas_copy = local_copy(master, mas, 3)
    mom_copy = local_copy(momentum, mom, 4)
    own_copies = [local_copy(deltas.at[:, core, :, columns(p)], own.at[:, :, columns(p)], 5 + p) for p in PARTS]
    tok_copies = [
        local_copy(tokens.at[pl.ds(i * TILE, TILE)], tok.at[pl.ds(i * TILE, TILE)], 8 + i) for i in range(4)]
    for copy in [steps_copy, bucket_copy] + own_copies + [gain_copy, mas_copy, mom_copy] + tok_copies:
        copy.start()

    barrier = pltpu.get_barrier_semaphore()
    peers = [sibling]
    for d in range(1, 8):
        k = lax.rem(chip + d, 8)
        peers.append(device(lax.div(x, 2) * 2 + lax.div(k, 4), lax.rem(k, 4), z, core))
    far = (1 - lax.div(x, 2)) * 2
    peers.append(device(far, y, z, core))
    peers.append(device(far + 1, y, z, core))
    for d in range(1, 4):
        peers.append(device(x, y, mod4(z + d), core))
    for peer in peers:
        pl.semaphore_signal(barrier, inc=1, device_id=peer, device_id_type=MESH)
    pl.semaphore_wait(barrier, len(peers))

    pair_copies = [
        pltpu.make_async_remote_copy(
            src_ref=deltas.at[:, 1 - core, :, columns(p)], dst_ref=sib.at[:, :, columns(p)],
            send_sem=pair_s.at[p], recv_sem=pair_r.at[p], device_id=sibling, device_id_type=MESH)
        for p in PARTS]
    for copy in pair_copies:
        copy.start()

    steps_copy.wait()
    bucket_copy.wait()
    counts = steps_v[...].astype(F32)
    share = counts / jnp.sum(counts, axis=0, keepdims=True)
    replica = lax.axis_index("rep")
    replica_ids = lax.broadcasted_iota(jnp.int32, (16, 16), 0)
    lane = lax.broadcasted_iota(jnp.int32, (ROWS, 128), 1)
    row = lax.broadcasted_iota(jnp.int32, (ROWS, 128), 0)
    mine = lane == row + core * ROWS
    buckets = bucket_v[...]
    for side, who in enumerate((replica, replica + 1 - 2 * core)):
        row_share = jnp.sum(jnp.where(replica_ids == who, share, 0.0), axis=0, keepdims=True)
        weight = jnp.zeros((8, 128), F32)
        for b in range(16):
            weight = weight + jnp.where(buckets == b, row_share[:, b:b + 1], 0.0)
        for k in range(8):
            column = jnp.sum(jnp.where(mine, weight[k:k + 1, :], 0.0), axis=1, keepdims=True)
            wcol[side, k] = jnp.broadcast_to(column, (ROWS, 128))

    def reduce_copy(part, d):
        k = lax.rem(chip + d, 8)
        return pltpu.make_async_remote_copy(
            src_ref=pairs.at[k, :, columns(part)], dst_ref=landed.at[d - 1, :, columns(part)],
            send_sem=red_s.at[part, d - 1], recv_sem=red_r.at[part, d - 1],
            device_id=device(lax.div(x, 2) * 2 + lax.div(k, 4), lax.rem(k, 4), z, core), device_id_type=MESH)

    for p in PARTS:
        own_copies[p].wait()
        pair_copies[p].wait_recv()

        @pl.loop(0, 8)
        def _(k):
            w0 = wcol[0, k][:, :1]
            w1 = wcol[1, k][:, :1]
            both = w0 * own[k, :, columns(p)].astype(F32) + w1 * sib[k, :, columns(p)].astype(F32)
            pairs[k, :, columns(p)] = both.astype(BF16)

        @pl.loop(1, 8)
        def _(d):
            reduce_copy(p, d).start()

    for ref in acc:
        ref[...] = jnp.zeros_like(ref)
    gain_copy.wait()
    gain_rows = gain_v[...].astype(F32).reshape(8, 128)
    gain_row = jnp.sum(
        jnp.where(lax.broadcasted_iota(jnp.int32, (8, 128), 0) == chip, gain_rows, 0.0), axis=0, keepdims=True)
    gain_col = jnp.sum(jnp.where(mine, gain_row, 0.0), axis=1, keepdims=True)
    mas_copy.wait()
    mom_copy.wait()
    for copy in tok_copies:
        copy.wait()

    @pl.loop(0, 1024 // 32)
    def _(i):
        rows = pl.ds(pl.multiple_of(i * 32, 32), 32)
        total = jnp.zeros((32, 128), F32)
        for j in range(64):
            v = tok[rows, j * 128:(j + 1) * 128].astype(F32)
            total = total + v * v
        mean = jnp.sum(total, axis=1, keepdims=True) * (1.0 / 8192.0)
        inv[rows, :] = jnp.broadcast_to(lax.rsqrt(mean + EPSILON), (32, 128))

    def place(part):
        return [here[q] for q in roles(part)]

    def along(axis, d):
        moved = [mod4(v + d) if q == axis else v for q, v in enumerate((x, y, z))]
        return device(*moved, core)

    def gather_copy(part, ref, index, target):
        return pltpu.make_async_remote_copy(
            src_ref=ref, dst_ref=ref, send_sem=gat_s.at[part, index], recv_sem=gat_r.at[part, index],
            device_id=target, device_id_type=MESH)

    def line_send(part, d):
        i1, i2, i3 = place(part)
        return gather_copy(part, layer[part].at[i3, i2, i1, core], LINE + d - 1, along(roles(part)[0], d))

    def line_recv(part, d):
        i1, i2, i3 = place(part)
        return gather_copy(part, layer[part].at[i3, i2, mod4(i1 - d), core], LINE + d - 1, sibling)

    def a_line(part, m, who):
        shift, j = item_place(m)
        i1, i2, i3 = place(part)
        return layer[part].at[mod4(i3 + shift), mod4(i2 - j), :, who]

    def plane_send(part, d):
        return gather_copy(part, a_line(part, 0, core), PLANE + d - 1, along(roles(part)[1], d))

    def plane_recv(part, d):
        return gather_copy(part, a_line(part, d, core), PLANE + d - 1, sibling)

    def cube_send(part, way, j):
        return gather_copy(part, a_line(part, j, core), CUBE + 2 * j + way, along(roles(part)[2], 1 - 2 * way))

    def cube_recv(part, m):
        return gather_copy(part, a_line(part, m, core), CUBE + m - 4, sibling)

    def forward_send(part, m):
        way = lax.rem(m, 2)
        return gather_copy(
            part, a_line(part, m, core), FORWARD + lax.div(m, 2) - 2, along(roles(part)[2], 1 - 2 * way))

    def forward_recv(part, m):
        return gather_copy(part, a_line(part, m, core), FORWARD + m - 12, sibling)

    def sibling_send(part, m):
        return gather_copy(part, a_line(part, m, core), SIBLING + m, sibling)

    def sibling_recv(part, m):
        return gather_copy(part, a_line(part, m, 1 - core), SIBLING + m, sibling)

    def multiply(part, m):
        q1, q2, q3 = roles(part)
        i1, i2, i3 = place(part)
        shift, j = item_place(m)
        spot = [None, None, None]
        spot[q2] = mod4(i2 - j)
        spot[q3] = mod4(i3 + shift)
        weights = layer[part][spot[q3], spot[q2]].reshape(8 * ROWS, SPANS[part][1])
        left = []
        for i in range(4):
            spot[q1] = i
            start = lax.div(spot[0], 2) * 4096 + spot[2] * 1024 + lax.rem(spot[0], 2) * 512 + spot[1] * 128
            left.append(tok[:, pl.ds(pl.multiple_of(start, 128), 128)])
        acc[part][...] += jnp.dot(jnp.concatenate(left, axis=1), weights, preferred_element_type=F32)

    for p in PARTS:
        @pl.loop(1, 8)
        def _(d):
            reduce_copy(p, d).wait_recv()

        averaged = pairs[chip, :, columns(p)].astype(F32)
        for d in range(7):
            averaged = averaged + landed[d, :, columns(p)].astype(F32)
        momentum_new = MOMENTUM_KEEP * mom[:, columns(p)] + averaged
        master_new = mas[:, columns(p)] - OUTER_RATE * (averaged + MOMENTUM_KEEP * momentum_new)
        mom[:, columns(p)] = momentum_new
        mas[:, columns(p)] = master_new
        i1, i2, i3 = place(p)
        layer[p][i3, i2, i1, core] = (gain_col * master_new).astype(BF16)
        for d in (1, 3, 2):
            line_send(p, d).start()

    mas_back = local_copy(mas, master_out, 3)
    mom_back = local_copy(mom, momentum_out, 4)
    mas_back.start()
    mom_back.start()

    @pl.loop(0, ITEMS + 1)
    def _(m):
        for p in PARTS:
            @pl.when(m == 0)
            def _():
                for d in (1, 3, 2):
                    line_recv(p, d).wait_recv()
                for d in (1, 3, 2):
                    plane_send(p, d).start()

            @pl.when((m >= 1) & (m < 4))
            def _():
                plane_recv(p, m).wait_recv()

            @pl.when(m < 4)
            def _():
                cube_send(p, 0, m).start()
                cube_send(p, 1, m).start()

            @pl.when((m >= 4) & (m < 12))
            def _():
                cube_recv(p, m).wait_recv()

                @pl.when(lax.rem(lax.div(m, 2), 2) == lax.rem(m, 2))
                def _():
                    forward_send(p, m).start()

            @pl.when((m >= 12) & (m < ITEMS))
            def _():
                forward_recv(p, m).wait_recv()

            @pl.when(m < ITEMS)
            def _():
                sibling_send(p, m).start()

            @pl.when(m >= 1)
            def _():
                sibling_recv(p, m - 1).wait_recv()
                multiply(p, m - 1)

    def keys_copy(t):
        rows = pl.ds(pl.multiple_of(t * TILE, TILE), TILE)
        return pltpu.make_async_copy(out.at[rows], keys.at[rows], local.at[8 + t])

    @pl.loop(0, 1024 // TILE)
    def _(t):
        rows = pl.ds(pl.multiple_of(t * TILE, TILE), TILE)
        scale = inv[rows, :][:, :1]
        for p in PARTS:
            out[rows, columns(p)] = (acc[p][rows, :] * scale).astype(BF16)
        keys_copy(t).start()

    for p in PARTS:
        pair_copies[p].wait_send()

        @pl.loop(1, 8)
        def _(d):
            reduce_copy(p, d).wait_send()

        @pl.loop(1, 4)
        def _(d):
            line_send(p, d).wait_send()
            plane_send(p, d).wait_send()

        @pl.loop(0, 4)
        def _(j):
            cube_send(p, 0, j).wait_send()
            cube_send(p, 1, j).wait_send()
            forward_send(p, 2 * j + 4).wait_send()

        @pl.loop(0, ITEMS)
        def _(m):
            sibling_send(p, m).wait_send()

    mas_back.wait()
    mom_back.wait()

    @pl.loop(0, 1024 // TILE)
    def _(t):
        keys_copy(t).wait()


def relay(keys, master_new, momentum_new, keys_out, master_out, momentum_out, done):
    copies = [
        pltpu.make_async_copy(keys.at[pl.ds(i * TILE, TILE)], keys_out.at[pl.ds(i * TILE, TILE)], done.at[i])
        for i in range(4)]
    copies.append(pltpu.make_async_copy(master_new, master_out, done.at[4]))
    copies.append(pltpu.make_async_copy(momentum_new, momentum_out, done.at[5]))
    for copy in copies:
        copy.start()
    for copy in copies:
        copy.wait()


def on_device(tokens, norm_gain, deltas, inner_steps, bucket_of_row, master, momentum):
    hbm = pl.BlockSpec(memory_space=pl.ANY)
    dma = pltpu.SemaphoreType.DMA
    shapes = (
        jax.ShapeDtypeStruct((1024, 1024), BF16),
        jax.ShapeDtypeStruct((ROWS, 1024), F32),
        jax.ShapeDtypeStruct((ROWS, 1024), F32),
    )
    results = pl.pallas_call(
        kernel,
        out_shape=shapes,
        in_specs=[hbm] * 7,
        out_specs=(hbm, hbm, hbm),
        scratch_shapes=[
            pltpu.VMEM((1024, 8192), BF16),
            *[pltpu.VMEM((4, 4, 4, 2, ROWS, width), BF16) for _, width in SPANS],
            *[pltpu.VMEM((1024, width), F32) for _, width in SPANS],
            pltpu.VMEM((8, ROWS, 1024), BF16),
            pltpu.VMEM((8, ROWS, 1024), BF16),
            pltpu.VMEM((8, ROWS, 1024), BF16),
            pltpu.VMEM((7, ROWS, 1024), BF16),
            pltpu.VMEM((ROWS, 1024), F32),
            pltpu.VMEM((ROWS, 1024), F32),
            pltpu.VMEM((1024,), BF16),
            pltpu.VMEM((16, 16), jnp.int32),
            pltpu.VMEM((8, 128), jnp.int32),
            pltpu.VMEM((2, 8, ROWS, 128), F32),
            pltpu.VMEM((1024, 128), F32),
            pltpu.VMEM((1024, 1024), BF16),
            dma((12,)),
            dma((3,)),
            dma((3,)),
            dma((3, 7)),
            dma((3, 7)),
            dma((3, COPIES)),
            dma((3, COPIES)),
        ],
        compiler_params=pltpu.CompilerParams(
            collective_id=0, has_side_effects=True, vmem_limit_bytes=50 * 1024 * 1024),
        cost_estimate=pl.CostEstimate(flops=2 * 1024 * 8192 * 1024, bytes_accessed=24 << 20, transcendentals=1024),
    )(
        *[pltpu.with_memory_space_constraint(v, pltpu.HBM) for v in (
        tokens,
        norm_gain,
        deltas.reshape(8, 2, ROWS, 1024),
        inner_steps,
        bucket_of_row.reshape(8, 128),
        master,
        momentum)],
    )
    return pl.pallas_call(
        relay,
        out_shape=shapes,
        in_specs=[pl.BlockSpec(memory_space=pltpu.VMEM)] * 3,
        out_specs=(hbm, hbm, hbm),
        scratch_shapes=[dma((6,))],
        compiler_params=pltpu.CompilerParams(vmem_limit_bytes=16 * 1024 * 1024),
    )(*results)


def solution(mesh):
    in_specs = (
        P(("rep", "fsdp"), None),
        P(),
        P("rep", "fsdp", None),
        P(),
        P("fsdp"),
        P(("fsdp", "rep"), None),
        P(("fsdp", "rep"), None),
    )
    out_specs = (P(("rep", "fsdp"), None), P(("fsdp", "rep"), None), P(("fsdp", "rep"), None))
    return jax.shard_map(
        on_device, mesh=mesh, in_specs=in_specs, out_specs=out_specs, check_vma=False
    )
```

```python
import jax
import jax.numpy as jnp
from jax import lax
from jax.experimental import pallas as pl
from jax.experimental.pallas import tpu as pltpu
from jax.sharding import PartitionSpec as P

OUTER_RATE = 0.7
MOMENTUM_KEEP = 0.9
EPSILON = 1e-05
MESH = pl.DeviceIdType.MESH
F32 = jnp.float32
BF16 = jnp.bfloat16

SPANS = ((0, 384), (384, 384), (768, 256))
ORDERS = ((1, 0, 2), (2, 1, 0), (0, 2, 1))
PARTS = range(3)
ROWS = 64
TILE = 256
LINE, PLANE, CUBE, FORWARD, SIBLING, COPIES = 0, 3, 6, 14, 18, 34
ITEMS = 16


def mod4(v):
    return lax.rem(v + 8, 4)


def position():
    rep = lax.axis_index("rep")
    fsdp = lax.axis_index("fsdp")
    x = lax.div(fsdp, 4) * 2 + lax.div(rep, 8)
    y = lax.rem(lax.div(rep, 2), 4)
    z = lax.rem(fsdp, 4)
    return x, y, z, lax.rem(rep, 2)


def device(x, y, z, core):
    return (lax.rem(x, 2) * 8 + y * 2 + core, lax.div(x, 2) * 4 + z)


def roles(part):
    return ORDERS[part]


def item_place(m):
    group = lax.div(m, 4)
    first, last = lax.div(3 - group, 3), lax.div(group, 3)
    middle = 1 - first - last
    shift = middle * (2 * lax.rem(m, 2) - 1) + 2 * last
    return shift, (first + last) * lax.rem(m, 4) + middle * (lax.div(m, 2) - 2)


def kernel(tokens, gain, deltas, steps, bucket, master, momentum,
           keys, master_out, momentum_out,
           tok, layer0, layer1, layer2, acc0, acc1, acc2, own, sib, pairs, landed, mas, mom, gain_v, steps_v, bucket_v,
           wcol, inv, out, local, pair_s, pair_r, red_s, red_r, gat_s, gat_r):
    layer = (layer0, layer1, layer2)
    acc = (acc0, acc1, acc2)
    here = position()
    x, y, z, core = here
    chip = lax.rem(x, 2) * 4 + y
    sibling = device(x, y, z, 1 - core)

    def columns(part):
        return pl.ds(*SPANS[part])

    def local_copy(src, dst, i):
        return pltpu.make_async_copy(src, dst, local.at[i])

    steps_copy = local_copy(steps, steps_v, 0)
    bucket_copy = local_copy(bucket, bucket_v, 1)
    gain_copy = local_copy(
        gain.at[pl.ds(pl.multiple_of(lax.axis_index("fsdp") * 1024, 1024), 1024)], gain_v, 2)
    mas_copy = local_copy(master, mas, 3)
    mom_copy = local_copy(momentum, mom, 4)
    own_copies = [local_copy(deltas.at[:, core, :, columns(p)], own.at[:, :, columns(p)], 5 + p) for p in PARTS]
    tok_copies = [
        local_copy(tokens.at[pl.ds(i * TILE, TILE)], tok.at[pl.ds(i * TILE, TILE)], 8 + i) for i in range(4)]
    for copy in [steps_copy, bucket_copy] + own_copies + [gain_copy, mas_copy, mom_copy] + tok_copies:
        copy.start()

    barrier = pltpu.get_barrier_semaphore()
    peers = [sibling]
    for d in range(1, 8):
        k = lax.rem(chip + d, 8)
        peers.append(device(lax.div(x, 2) * 2 + lax.div(k, 4), lax.rem(k, 4), z, core))
    far = (1 - lax.div(x, 2)) * 2
    peers.append(device(far, y, z, core))
    peers.append(device(far + 1, y, z, core))
    for d in range(1, 4):
        peers.append(device(x, y, mod4(z + d), core))
    for peer in peers:
        pl.semaphore_signal(barrier, inc=1, device_id=peer, device_id_type=MESH)
    pl.semaphore_wait(barrier, len(peers))

    pair_copies = [
        pltpu.make_async_remote_copy(
            src_ref=deltas.at[:, 1 - core, :, columns(p)], dst_ref=sib.at[:, :, columns(p)],
            send_sem=pair_s.at[p], recv_sem=pair_r.at[p], device_id=sibling, device_id_type=MESH)
        for p in PARTS]
    for copy in pair_copies:
        copy.start()

    steps_copy.wait()
    bucket_copy.wait()
    counts = steps_v[...].astype(F32)
    share = counts / jnp.sum(counts, axis=0, keepdims=True)
    replica = lax.axis_index("rep")
    replica_ids = lax.broadcasted_iota(jnp.int32, (16, 16), 0)
    lane = lax.broadcasted_iota(jnp.int32, (ROWS, 128), 1)
    row = lax.broadcasted_iota(jnp.int32, (ROWS, 128), 0)
    mine = lane == row + core * ROWS
    buckets = bucket_v[...]
    for side, who in enumerate((replica, replica + 1 - 2 * core)):
        row_share = jnp.sum(jnp.where(replica_ids == who, share, 0.0), axis=0, keepdims=True)
        weight = jnp.zeros((8, 128), F32)
        for b in range(16):
            weight = weight + jnp.where(buckets == b, row_share[:, b:b + 1], 0.0)
        for k in range(8):
            column = jnp.sum(jnp.where(mine, weight[k:k + 1, :], 0.0), axis=1, keepdims=True)
            wcol[side, k] = jnp.broadcast_to(column, (ROWS, 128))

    def reduce_copy(part, d):
        k = lax.rem(chip + d, 8)
        return pltpu.make_async_remote_copy(
            src_ref=pairs.at[k, :, columns(part)], dst_ref=landed.at[d - 1, :, columns(part)],
            send_sem=red_s.at[part, d - 1], recv_sem=red_r.at[part, d - 1],
            device_id=device(lax.div(x, 2) * 2 + lax.div(k, 4), lax.rem(k, 4), z, core), device_id_type=MESH)

    for p in PARTS:
        own_copies[p].wait()
        pair_copies[p].wait_recv()

        @pl.loop(0, 8)
        def _(k):
            w0 = wcol[0, k][:, :1]
            w1 = wcol[1, k][:, :1]
            both = w0 * own[k, :, columns(p)].astype(F32) + w1 * sib[k, :, columns(p)].astype(F32)
            pairs[k, :, columns(p)] = both.astype(BF16)

        @pl.loop(1, 8)
        def _(d):
            reduce_copy(p, d).start()

    for ref in acc:
        ref[...] = jnp.zeros_like(ref)
    gain_copy.wait()
    gain_rows = gain_v[...].astype(F32).reshape(8, 128)
    gain_row = jnp.sum(
        jnp.where(lax.broadcasted_iota(jnp.int32, (8, 128), 0) == chip, gain_rows, 0.0), axis=0, keepdims=True)
    gain_col = jnp.sum(jnp.where(mine, gain_row, 0.0), axis=1, keepdims=True)
    mas_copy.wait()
    mom_copy.wait()
    for copy in tok_copies:
        copy.wait()

    @pl.loop(0, 1024 // 32)
    def _(i):
        rows = pl.ds(pl.multiple_of(i * 32, 32), 32)
        total = jnp.zeros((32, 128), F32)
        for j in range(64):
            v = tok[rows, j * 128:(j + 1) * 128].astype(F32)
            total = total + v * v
        mean = jnp.sum(total, axis=1, keepdims=True) * (1.0 / 8192.0)
        inv[rows, :] = jnp.broadcast_to(lax.rsqrt(mean + EPSILON), (32, 128))

    def place(part):
        return [here[q] for q in roles(part)]

    def along(axis, d):
        moved = [mod4(v + d) if q == axis else v for q, v in enumerate((x, y, z))]
        return device(*moved, core)

    def gather_copy(part, ref, index, target):
        return pltpu.make_async_remote_copy(
            src_ref=ref, dst_ref=ref, send_sem=gat_s.at[part, index], recv_sem=gat_r.at[part, index],
            device_id=target, device_id_type=MESH)

    def line_send(part, d):
        i1, i2, i3 = place(part)
        return gather_copy(part, layer[part].at[i3, i2, i1, core], LINE + d - 1, along(roles(part)[0], d))

    def line_recv(part, d):
        i1, i2, i3 = place(part)
        return gather_copy(part, layer[part].at[i3, i2, mod4(i1 - d), core], LINE + d - 1, sibling)

    def a_line(part, m, who):
        shift, j = item_place(m)
        i1, i2, i3 = place(part)
        return layer[part].at[mod4(i3 + shift), mod4(i2 - j), :, who]

    def plane_send(part, d):
        return gather_copy(part, a_line(part, 0, core), PLANE + d - 1, along(roles(part)[1], d))

    def plane_recv(part, d):
        return gather_copy(part, a_line(part, d, core), PLANE + d - 1, sibling)

    def cube_send(part, way, j):
        return gather_copy(part, a_line(part, j, core), CUBE + 2 * j + way, along(roles(part)[2], 1 - 2 * way))

    def cube_recv(part, m):
        return gather_copy(part, a_line(part, m, core), CUBE + m - 4, sibling)

    def forward_send(part, m):
        way = lax.rem(m, 2)
        return gather_copy(
            part, a_line(part, m, core), FORWARD + lax.div(m, 2) - 2, along(roles(part)[2], 1 - 2 * way))

    def forward_recv(part, m):
        return gather_copy(part, a_line(part, m, core), FORWARD + m - 12, sibling)

    def sibling_send(part, m):
        return gather_copy(part, a_line(part, m, core), SIBLING + m, sibling)

    def sibling_recv(part, m):
        return gather_copy(part, a_line(part, m, 1 - core), SIBLING + m, sibling)

    def multiply(part, m):
        q1, q2, q3 = roles(part)
        i1, i2, i3 = place(part)
        shift, j = item_place(m)
        spot = [None, None, None]
        spot[q2] = mod4(i2 - j)
        spot[q3] = mod4(i3 + shift)
        weights = layer[part][spot[q3], spot[q2]].reshape(8 * ROWS, SPANS[part][1])
        left = []
        for i in range(4):
            spot[q1] = i
            start = lax.div(spot[0], 2) * 4096 + spot[2] * 1024 + lax.rem(spot[0], 2) * 512 + spot[1] * 128
            left.append(tok[:, pl.ds(pl.multiple_of(start, 128), 128)])
        acc[part][...] += jnp.dot(jnp.concatenate(left, axis=1), weights, preferred_element_type=F32)

    for p in PARTS:
        @pl.loop(1, 8)
        def _(d):
            reduce_copy(p, d).wait_recv()

        averaged = pairs[chip, :, columns(p)].astype(F32)
        for d in range(7):
            averaged = averaged + landed[d, :, columns(p)].astype(F32)
        momentum_new = MOMENTUM_KEEP * mom[:, columns(p)] + averaged
        master_new = mas[:, columns(p)] - OUTER_RATE * (averaged + MOMENTUM_KEEP * momentum_new)
        mom[:, columns(p)] = momentum_new
        mas[:, columns(p)] = master_new
        i1, i2, i3 = place(p)
        layer[p][i3, i2, i1, core] = (gain_col * master_new).astype(BF16)
        for d in (1, 3, 2):
            line_send(p, d).start()

    mas_back = local_copy(mas, master_out, 3)
    mom_back = local_copy(mom, momentum_out, 4)
    mas_back.start()
    mom_back.start()

    @pl.loop(0, ITEMS + 1)
    def _(m):
        for p in (2, 0, 1):
            @pl.when(m == 0)
            def _():
                for d in (1, 3, 2):
                    line_recv(p, d).wait_recv()
                for d in (1, 3, 2):
                    plane_send(p, d).start()

            @pl.when((m >= 1) & (m < 4))
            def _():
                plane_recv(p, m).wait_recv()

            @pl.when(m < 4)
            def _():
                cube_send(p, 0, m).start()
                cube_send(p, 1, m).start()

            @pl.when((m >= 4) & (m < 12))
            def _():
                cube_recv(p, m).wait_recv()

                @pl.when(lax.rem(lax.div(m, 2), 2) == lax.rem(m, 2))
                def _():
                    forward_send(p, m).start()

            @pl.when((m >= 12) & (m < ITEMS))
            def _():
                forward_recv(p, m).wait_recv()

            @pl.when(m < ITEMS)
            def _():
                sibling_send(p, m).start()

            @pl.when(m >= 1)
            def _():
                sibling_recv(p, m - 1).wait_recv()
                multiply(p, m - 1)

    def keys_copy(t):
        rows = pl.ds(pl.multiple_of(t * TILE, TILE), TILE)
        return pltpu.make_async_copy(out.at[rows], keys.at[rows], local.at[8 + t])

    @pl.loop(0, 1024 // TILE)
    def _(t):
        rows = pl.ds(pl.multiple_of(t * TILE, TILE), TILE)
        scale = inv[rows, :][:, :1]
        for p in PARTS:
            out[rows, columns(p)] = (acc[p][rows, :] * scale).astype(BF16)
        keys_copy(t).start()

    for p in PARTS:
        pair_copies[p].wait_send()

        @pl.loop(1, 8)
        def _(d):
            reduce_copy(p, d).wait_send()

        @pl.loop(1, 4)
        def _(d):
            line_send(p, d).wait_send()
            plane_send(p, d).wait_send()

        @pl.loop(0, 4)
        def _(j):
            cube_send(p, 0, j).wait_send()
            cube_send(p, 1, j).wait_send()
            forward_send(p, 2 * j + 4).wait_send()

        @pl.loop(0, ITEMS)
        def _(m):
            sibling_send(p, m).wait_send()

    mas_back.wait()
    mom_back.wait()

    @pl.loop(0, 1024 // TILE)
    def _(t):
        keys_copy(t).wait()


def relay(keys, master_new, momentum_new, keys_out, master_out, momentum_out, done):
    copies = [
        pltpu.make_async_copy(keys.at[pl.ds(i * TILE, TILE)], keys_out.at[pl.ds(i * TILE, TILE)], done.at[i])
        for i in range(4)]
    copies.append(pltpu.make_async_copy(master_new, master_out, done.at[4]))
    copies.append(pltpu.make_async_copy(momentum_new, momentum_out, done.at[5]))
    for copy in copies:
        copy.start()
    for copy in copies:
        copy.wait()


def on_device(tokens, norm_gain, deltas, inner_steps, bucket_of_row, master, momentum):
    hbm = pl.BlockSpec(memory_space=pl.ANY)
    dma = pltpu.SemaphoreType.DMA
    shapes = (
        jax.ShapeDtypeStruct((1024, 1024), BF16),
        jax.ShapeDtypeStruct((ROWS, 1024), F32),
        jax.ShapeDtypeStruct((ROWS, 1024), F32),
    )
    results = pl.pallas_call(
        kernel,
        out_shape=shapes,
        in_specs=[hbm] * 7,
        out_specs=(hbm, hbm, hbm),
        scratch_shapes=[
            pltpu.VMEM((1024, 8192), BF16),
            *[pltpu.VMEM((4, 4, 4, 2, ROWS, width), BF16) for _, width in SPANS],
            *[pltpu.VMEM((1024, width), F32) for _, width in SPANS],
            pltpu.VMEM((8, ROWS, 1024), BF16),
            pltpu.VMEM((8, ROWS, 1024), BF16),
            pltpu.VMEM((8, ROWS, 1024), BF16),
            pltpu.VMEM((7, ROWS, 1024), BF16),
            pltpu.VMEM((ROWS, 1024), F32),
            pltpu.VMEM((ROWS, 1024), F32),
            pltpu.VMEM((1024,), BF16),
            pltpu.VMEM((16, 16), jnp.int32),
            pltpu.VMEM((8, 128), jnp.int32),
            pltpu.VMEM((2, 8, ROWS, 128), F32),
            pltpu.VMEM((1024, 128), F32),
            pltpu.VMEM((1024, 1024), BF16),
            dma((12,)),
            dma((3,)),
            dma((3,)),
            dma((3, 7)),
            dma((3, 7)),
            dma((3, COPIES)),
            dma((3, COPIES)),
        ],
        compiler_params=pltpu.CompilerParams(
            collective_id=0, has_side_effects=True, vmem_limit_bytes=50 * 1024 * 1024),
        cost_estimate=pl.CostEstimate(flops=2 * 1024 * 8192 * 1024, bytes_accessed=24 << 20, transcendentals=1024),
    )(
        *[pltpu.with_memory_space_constraint(v, pltpu.HBM) for v in (
        tokens,
        norm_gain,
        deltas.reshape(8, 2, ROWS, 1024),
        inner_steps,
        bucket_of_row.reshape(8, 128),
        master,
        momentum)],
    )
    return pl.pallas_call(
        relay,
        out_shape=shapes,
        in_specs=[pl.BlockSpec(memory_space=pltpu.VMEM)] * 3,
        out_specs=(hbm, hbm, hbm),
        scratch_shapes=[dma((6,))],
        compiler_params=pltpu.CompilerParams(vmem_limit_bytes=16 * 1024 * 1024),
    )(*results)


def solution(mesh):
    in_specs = (
        P(("rep", "fsdp"), None),
        P(),
        P("rep", "fsdp", None),
        P(),
        P("fsdp"),
        P(("fsdp", "rep"), None),
        P(("fsdp", "rep"), None),
    )
    out_specs = (P(("rep", "fsdp"), None), P(("fsdp", "rep"), None), P(("fsdp", "rep"), None))
    return jax.shard_map(
        on_device, mesh=mesh, in_specs=in_specs, out_specs=out_specs, check_vma=False
    )
```
